256 devices in a mesh: tile: 64 (over x, z, core), tm: 4 (over y).
Axes of the slice: x: 4, y: 4, z: 8, core: 2. Of those that a mesh axis runs over, the one named last changes fastest.
Arguments:
- movie_frames: bfloat16 [512, 262144], P(('tile', 'tm')), as said below
- footprints: bfloat16 [64, 4096, 256], P('tile')
- tile_blocks: int32 [64, 16], P('tile'), may hold values from 0 to 63, as said below
- tile_count: int32 [64], P('tile'), may hold values from 1 to 16
- traces: bfloat16 [1024, 512], P('tile', 'tm'), may hold values from 0 to 2
Outputs:
- new_traces: float32 [1024, 512], P('tile', 'tm')
The draws below stay inside these ranges and needn't reach their ends.
Inputs may be any that keep to these rules, and one draw needn't show every extreme that they name: `tile_blocks`: slot 0 of tile t names block t; the 16 blocks listed for one tile are distinct; slots at or past tile_count of a tile are ignored. For every tile g and every other tile h != g, tile g lists block h at most once (blocks are owned one per tile). `movie_frames`: fluorescence values, frame by frame.
All inputs are finite; a program needn't handle non-finite values.
Results may differ from the reference program's by a relative error of at most 0.0003.
Values may be sent and summed in bfloat16 or wider, within the bound.
A program may use at most 64 MiB of HBM per device.

```python
import jax
import jax.numpy as jnp
from jax import lax

TILE_PX = 4096
NB = 16
SLOTS = 16
TILES_DEV = 1
TILES = 64
NEURONS = 1024
FRAMES = 512
OWNER_CAP = 1


def draw_footprints(key, part):
    first_key, second_key = jax.random.split(jax.random.fold_in(key, 11))
    shape = (TILES, TILE_PX, SLOTS * NB)
    scale_factor = 1.0 / (0.2125 * SLOTS * NB)
    values = jax.random.uniform(first_key, shape, jnp.float32, 0.5, 1.5)
    support = jax.random.bernoulli(second_key, 0.125, shape).astype(jnp.float32)
    return (scale_factor * values * (0.1 + 0.9 * support)).astype(jnp.bfloat16)


def listed_blocks(key):
    base_key = jax.random.fold_in(key, 23)
    device_total = TILES // TILES_DEV
    other_total = device_total - 1
    menu_size = other_total * OWNER_CAP + TILES_DEV - 1
    tail_size = menu_size - OWNER_CAP

    def one_device(device):
        device_key = jax.random.fold_in(base_key, device)
        owner_order = jax.random.permutation(jax.random.fold_in(device_key, 1), other_total).astype(jnp.int32)
        owners = owner_order + (owner_order >= device).astype(jnp.int32)
        pick_keys = jax.random.split(jax.random.fold_in(device_key, 2), other_total)
        local_picks = jax.vmap(lambda pick_key: jax.random.permutation(pick_key, TILES_DEV)[:OWNER_CAP])(pick_keys)
        remote_blocks = (owners[:, None] * TILES_DEV + local_picks.astype(jnp.int32)).reshape(-1)

        def one_tile(local_tile):
            tile_key = jax.random.fold_in(device_key, 3 + local_tile)
            spare_blocks = jnp.arange(TILES_DEV - 1, dtype=jnp.int32)
            spare_blocks = spare_blocks + (spare_blocks >= local_tile).astype(jnp.int32)
            menu_blocks = jnp.concatenate([remote_blocks, device * TILES_DEV + spare_blocks])
            first_key, second_key = jax.random.split(tile_key)
            forced = jnp.concatenate([jnp.arange(OWNER_CAP, dtype=jnp.int32), OWNER_CAP + jax.random.permutation(first_key, tail_size).astype(jnp.int32)])
            free_order = jax.random.permutation(second_key, menu_size).astype(jnp.int32)
            order_used = jnp.where(local_tile == 0, forced, free_order)[:SLOTS - 1]
            own_block = (device * TILES_DEV + local_tile).astype(jnp.int32)
            return jnp.concatenate([own_block[None], menu_blocks[order_used]])
        return jax.vmap(one_tile)(jnp.arange(TILES_DEV, dtype=jnp.int32))
    all_rows = jax.vmap(one_device)(jnp.arange(device_total, dtype=jnp.int32))
    return all_rows.reshape(TILES, SLOTS).astype(jnp.int32)


def draw_tile_blocks(key, part):
    return listed_blocks(key)


def draw_movie_frames(key, part):
    footprint_all = draw_footprints(key, part)
    block_list = listed_blocks(key)
    activity_key = jax.random.fold_in(jax.random.fold_in(key, 37), 0)
    noise_key = jax.random.fold_in(jax.random.fold_in(key, 37), 2)
    activity = jax.random.uniform(activity_key, (TILES, NB, FRAMES), jnp.float32, 0.0, 2.0)

    def one_tile(tile_index):
        chosen = jnp.take(activity, block_list[tile_index], axis=0).reshape(SLOTS * NB, FRAMES)
        footprint = footprint_all[tile_index].astype(jnp.float32)
        clean_movie = jnp.dot(footprint, chosen, precision=lax.Precision.HIGHEST)
        tile_key = jax.random.fold_in(noise_key, tile_index)
        noise_part = 0.05 * jnp.clip(jax.random.normal(tile_key, (TILE_PX, FRAMES), jnp.float32), -3.0, 3.0)
        return (clean_movie + noise_part).astype(jnp.bfloat16)
    tile_movies = lax.map(one_tile, jnp.arange(TILES, dtype=jnp.int32))
    return tile_movies.transpose(2, 0, 1).reshape(FRAMES, TILES * TILE_PX)


def set_ends(entries, key, least, top_value):
    shape = entries.shape
    place = [jax.random.randint(jax.random.fold_in(key, axis), (), 0, shape[axis]) for axis in range(len(shape))]
    entries = entries.at[tuple(place)].set(least)
    longest = shape.index(max(shape))
    place[longest] = (place[longest] + 1) % shape[longest]
    return entries.at[tuple(place)].set(top_value)


def block_scale(key, shape, pieces, low, top_value):
    def one(axis_at, shards_of):
        draws = jax.random.uniform(jax.random.fold_in(jax.random.fold_in(key, 6), axis_at), (shards_of,), jnp.float32, low / len(pieces), top_value / len(pieces))
        return jnp.repeat(jnp.exp(draws), shape[axis_at] // shards_of).reshape((-1,) + (1,) * (len(shape) - axis_at - 1))

    gain = one(*pieces[0])
    for cut in pieces[1:]:
        gain = gain * one(*cut)
    return gain


def setup_inputs(seed: int = 0) -> dict:
    streams_of = jax.random.split(jax.random.key(seed), 6)
    return {
        "movie_frames": draw_movie_frames(jax.random.fold_in(streams_of[5], 71), 0),
        "footprints": draw_footprints(jax.random.fold_in(streams_of[5], 71), 0),
        "tile_blocks": draw_tile_blocks(jax.random.fold_in(streams_of[5], 71), 0),
        "tile_count": set_ends(jax.random.randint(streams_of[3], (TILES,), 1, SLOTS + 1), jax.random.fold_in(streams_of[3], 1), 1, SLOTS).astype(jnp.int32),
        "traces": jnp.clip(2.0 * jax.random.uniform(streams_of[4], (NEURONS, FRAMES), jnp.float32) ** block_scale(streams_of[4], (NEURONS, FRAMES), ((0, 64), (1, 4)), -0.2, 0.2), 0.0, 2.0).astype(jnp.bfloat16),
    }


def update_traces(quotient, block_gram, previous):
    change = jnp.zeros(previous.shape, jnp.float32)
    updated_rows = []
    for neuron in range(previous.shape[1]):
        coupling = jnp.einsum("bj,bjf->bf", block_gram[:, neuron, :], change, precision=lax.Precision.HIGHEST)
        increment = (quotient[:, neuron] - coupling) / block_gram[:, neuron, neuron][:, None]
        updated = jnp.maximum(previous[:, neuron] + increment, 0.0)
        change = change.at[:, neuron].set(updated - previous[:, neuron])
        updated_rows.append(updated)
    return jnp.stack(updated_rows, axis=1)


def reference(movie_frames, footprints, tile_blocks, tile_count, traces):
    frames = movie_frames.shape[0]
    movie_tiles = movie_frames.reshape(frames, TILES, TILE_PX)
    trace_table = traces.reshape(TILES, NB, frames)
    slot_index = jnp.arange(SLOTS, dtype=jnp.int32)

    def one_tile(totals, tile_index):
        quotient, block_gram = totals
        blocks = tile_blocks[tile_index]
        live_slots = slot_index < tile_count[tile_index]
        chosen = jnp.where(live_slots[:, None, None], trace_table[blocks], jnp.zeros((), traces.dtype))
        chosen = chosen.reshape(SLOTS * NB, frames)
        footprint = footprints[tile_index]
        model_rows = lax.dot_general(chosen, footprint, (((0,), (1,)), ((), ())), preferred_element_type=jnp.float32)
        frame_rows = lax.dynamic_index_in_dim(movie_tiles, tile_index, 1, keepdims=False)
        residual = (frame_rows.astype(jnp.float32) - model_rows).astype(jnp.bfloat16)
        partial_rows = lax.dot_general(footprint, residual, (((0,), (1,)), ((), ())), preferred_element_type=jnp.float32)
        partial_rows = jnp.where(live_slots[:, None, None], partial_rows.reshape(SLOTS, NB, frames), 0.0)
        footprint_wide = footprint.astype(jnp.float32).reshape(TILE_PX, SLOTS, NB)
        gram_block = jnp.einsum("psi,psj->sij", footprint_wide, footprint_wide, precision=lax.Precision.HIGHEST)
        gram_block = jnp.where(live_slots[:, None, None], gram_block, 0.0)
        return (quotient.at[blocks].add(partial_rows), block_gram.at[blocks].add(gram_block)), None

    start_totals = (jnp.zeros((TILES, NB, frames), jnp.float32), jnp.zeros((TILES, NB, NB), jnp.float32))
    (quotient, block_gram), _ = lax.scan(one_tile, start_totals, jnp.arange(TILES, dtype=jnp.int32))
    previous = traces.astype(jnp.float32).reshape(TILES, NB, frames)
    return update_traces(quotient, block_gram, previous).reshape(TILES * NB, frames)
```

```python
import functools

import jax
import jax.numpy as jnp
from jax import lax
from jax.experimental import pallas as pl
from jax.experimental.pallas import tpu as pltpu
from jax.sharding import PartitionSpec as P

MESH = pl.DeviceIdType.MESH
NX, NY, NZ, NC = 4, 4, 8, 2
NB, SLOTS, LANES = 16, 16, 128
ROWS = NY * 2 * NC
FAR_FIRST = (4, 3, 5, 2, 6, 1, 7, 0)


def remote(src, dst, send, recv, device):
    return pltpu.make_async_remote_copy(
        src_ref=src, dst_ref=dst, send_sem=send, recv_sem=recv, device_id=device, device_id_type=MESH
    )


def kernel(
    blocks, count, movie, feet, traces, out,
    f_v, arrived, model, resid, table, chosen, gfull, diag, inverse, part,
    gs1, gr1, gs2, gr2, gs3, gr3, gcol, ps1, pr1, ps2, pr2, ps3, pr3,
    f_sem, ms, mr, tzs, tzr, txs, txr, tcs, tcr,
    gcs, gcr, gxs, gxr, gzs, gzr, pcs, pcr, pxs, pxr, pzs, pzr,
):
    t = lax.axis_index("tile")
    y = lax.axis_index("tm")
    x = t // 16
    z = lax.rem(t // 2, 8)
    c = lax.rem(t, 2)
    pixels = f_v.shape[0]
    col_tiles = arrived.shape[1]

    def line_x(d):
        return lax.rem(x + d, NX)

    def line_z(d):
        return lax.rem(z + d, NZ)

    def at(x_, z_, c_):
        return (x_ * 16 + z_ * 2 + c_, y)

    f_copy = pltpu.make_async_copy(feet, f_v, f_sem)
    f_copy.start()

    barrier = pltpu.get_barrier_semaphore()
    for d in (4, 3, 5, 2, 6, 1, 7):
        pl.semaphore_signal(barrier, inc=1, device_id=at(x, line_z(d), c), device_id_type=MESH)
    for d in (2, 1, 3):
        pl.semaphore_signal(barrier, inc=1, device_id=at(line_x(d), z, c), device_id_type=MESH)
    pl.semaphore_signal(barrier, inc=1, device_id=at(x, z, 1 - c), device_id_type=MESH)

    def greet(k, carry):
        source_tile = y * 16 + k // 4
        source_tm = lax.rem(k, 4)

        @pl.when(jnp.logical_or(source_tile != t, source_tm != y))
        def _():
            pl.semaphore_signal(
                barrier, inc=1, device_id=(source_tile, source_tm), device_id_type=MESH
            )

        return carry

    lax.fori_loop(0, 64, greet, 0)

    f_copy.wait()

    def gram_step(i, acc):
        rows = f_v[pl.ds(pl.multiple_of(i * 512, 512), 512), :]
        return acc + lax.dot_general(
            rows, rows, (((0,), (0,)), ((), ())), preferred_element_type=jnp.float32
        )

    gfull[...] = lax.fori_loop(
        0, pixels // 512, gram_step, jnp.zeros((SLOTS * NB, SLOTS * NB), jnp.float32)
    )
    lane = lax.broadcasted_iota(jnp.int32, (NB, LANES), 1)
    lane_block = lane // NB

    def spread(value):
        value = value + pltpu.roll(value, 16, 1)
        value = value + pltpu.roll(value, 32, 1)
        return value + pltpu.roll(value, 64, 1)

    for s in range(SLOTS):
        lanes = gfull[s * NB : (s + 1) * NB, (s // 8) * LANES : (s // 8 + 1) * LANES]
        diag[s] = spread(jnp.where(lane_block == s % 8, lanes, 0.0))

    live_count = count[0]
    place = []
    for s in range(SLOTS):
        b = blocks[0, s]
        where_ = (b // 16) * 16 + lax.rem(b, 2) * 8 + lax.rem(b // 2, 8)
        place.append(jnp.where(s < live_count, where_, -1))

    def find(d, carry):
        found = jnp.int32(0)
        for s in range(SLOTS):
            found = found + jnp.where(place[s] == d, s + 1, 0)
        inverse[d] = found
        return carry

    lax.fori_loop(0, 64, find, 0)

    self_here = (x == y).astype(jnp.int32)
    pl.semaphore_wait(barrier, 64 - self_here + 11)

    table[x, c, z] = traces[...]
    t_z = []
    for i, d in enumerate((4, 3, 5, 2, 6, 1, 7)):
        cp = remote(traces, table.at[x, c, z], tzs.at[i], tzr.at[z], at(x, line_z(d), c))
        cp.start()
        t_z.append(cp)

    def send_movie(k, carry):
        order = k // 8
        rest = lax.rem(k, 8)
        half = (order + 1) // 2
        dz = jnp.where(lax.rem(order, 2) == 0, 4 + half, 4 - half)
        dz = jnp.where(order == 0, 4, dz)
        to = lax.rem(x + rest // 2, NX) * 16 + lax.rem(z + dz, NZ) * 2 + lax.rem(c + rest, 2)
        here = jnp.logical_and(to == t, x == y)
        landing = arrived.at[z, :, c * 4 + y]

        @pl.when(jnp.logical_not(here))
        def _():
            remote(movie.at[to], landing, ms, mr.at[z], (to, x)).start()

        @pl.when(here)
        def _():
            pltpu.make_async_copy(movie.at[to], landing, mr.at[z]).start()

        return carry

    lax.fori_loop(0, 16, send_movie, 0)

    def wait_recv(dst, sem):
        remote(dst, dst, sem, sem, (t, y)).wait_recv()

    for d in range(1, NZ):
        wait_recv(table.at[x, c, line_z(d)], tzr.at[line_z(d)])
    t_x = []
    for i, d in enumerate((2, 1, 3)):
        cp = remote(table.at[x, c], table.at[x, c], txs.at[i], txr.at[x], at(line_x(d), z, c))
        cp.start()
        t_x.append(cp)

    def packed(x_, c_):
        total = jnp.zeros((NB, LANES), jnp.float32)
        for z_ in range(NZ):
            slot = inverse[x_ * 16 + c_ * 8 + z_]
            value = diag[jnp.maximum(slot - 1, 0)]
            total = total + jnp.where(
                jnp.logical_and(lane_block == z_, slot > 0), value, 0.0
            )
        return total

    for x_ in range(NX):
        gs1[x_] = packed(x_, 1 - c)
    g_c = remote(gs1, gr1, gcs, gcr, at(x, z, 1 - c))
    g_c.start()

    lax.fori_loop(16, 40, send_movie, 0)

    for d in (2, 1, 3):
        wait_recv(table.at[line_x(d), c], txr.at[line_x(d)])
    t_c = remote(table.at[:, c], table.at[:, c], tcs, tcr, at(x, z, 1 - c))
    t_c.start()

    g_c.wait_recv()
    g_x = []
    for i, d in enumerate((2, 1, 3)):
        gs2[i] = packed(line_x(d), c) + gr1[line_x(d)]
        cp = remote(gs2.at[i], gr2.at[x], gxs.at[i], gxr.at[x], at(line_x(d), z, c))
        cp.start()
        g_x.append(cp)
    g_own = packed(x, c) + gr1[x]

    lax.fori_loop(40, 64, send_movie, 0)

    wait_recv(table.at[:, 1 - c], tcr)
    for s in range(SLOTS):
        b = blocks[0, s]
        value = table[b // 16, lax.rem(b, 2), lax.rem(b // 2, 8)]
        chosen[s * NB : (s + 1) * NB, :] = jnp.where(
            s < live_count, value.astype(jnp.float32), 0.0
        )
    picked = jnp.transpose(chosen[...]).astype(jnp.bfloat16)

    def model_step(i, carry):
        at_ = pl.ds(pl.multiple_of(i * 512, 512), 512)
        model[:, at_] = lax.dot_general(
            picked, f_v[at_, :], (((1,), (1,)), ((), ())), preferred_element_type=jnp.float32
        )
        return carry

    lax.fori_loop(0, pixels // 512, model_step, 0)

    for d in (2, 1, 3):
        wait_recv(gr2.at[line_x(d)], gxr.at[line_x(d)])
        g_own = g_own + gr2[line_x(d)]
    gs3[...] = g_own
    g_z = []
    for i, d in enumerate((4, 3, 5, 2, 6, 1, 7)):
        cp = remote(gs3, gr3.at[z], gzs.at[i], gzr.at[z], at(x, line_z(d), c))
        cp.start()
        g_z.append(cp)

    for d in FAR_FIRST:
        zs = lax.rem(z + NZ - d, NZ)
        wait_recv(arrived.at[zs], mr.at[zs])
        rows = pl.ds(pl.multiple_of(zs * ROWS, ROWS), ROWS)

        def residual_step(j, carry):
            for i in range(4):
                col = pl.ds(pl.multiple_of(j * 512, 512) + i * LANES, LANES)
                frames = arrived[zs, j * 4 + i].reshape(ROWS, LANES).astype(jnp.float32)
                resid[rows, col] = (frames - model[rows, col]).astype(jnp.bfloat16)
            return carry

        lax.fori_loop(0, col_tiles // 4, residual_step, 0)

    for d in range(1, NZ):
        wait_recv(gr3.at[line_z(d)], gzr.at[line_z(d)])
        g_own = g_own + gr3[line_z(d)]
    g_own = spread(jnp.where(lane_block == z, g_own, 0.0))
    for k in range(NB):
        column = jnp.sum(jnp.where(lane == k, g_own, 0.0), axis=1, keepdims=True)
        gcol[k] = jnp.broadcast_to(column, (NB, LANES))

    product = jnp.dot(resid[...], f_v[...], preferred_element_type=jnp.float32)
    part[...] = jnp.transpose(product).reshape(SLOTS, NB, LANES)

    def block_for(d):
        slot = inverse[d]
        return jnp.where(slot > 0, part[jnp.maximum(slot - 1, 0)], 0.0)

    p_c = []
    for x_ in range(NX):
        for z_ in range(NZ):
            ps1[x_, z_] = block_for(x_ * 16 + (1 - c) * 8 + z_)
        cp = remote(ps1.at[x_], pr1.at[x_], pcs.at[x_], pcr.at[x_], at(x, z, 1 - c))
        cp.start()
        p_c.append(cp)
    p_x = []
    for i, d in enumerate((2, 1, 3, 0)):
        xd = line_x(d)
        wait_recv(pr1.at[xd], pcr.at[xd])
        for z_ in range(NZ):
            ps2[i, z_] = pr1[xd, z_] + block_for(xd * 16 + c * 8 + z_)
        if d:
            cp = remote(ps2.at[i], pr2.at[x], pxs.at[i], pxr.at[x], at(xd, z, c))
            cp.start()
            p_x.append(cp)
    for d in (1, 3, 2):
        wait_recv(pr2.at[line_x(d)], pxr.at[line_x(d)])
    p_z = []
    quotient = None
    for i, d in enumerate(FAR_FIRST):
        zd = line_z(d)
        value = ps2[3, zd] + pr2[line_x(1), zd] + pr2[line_x(2), zd] + pr2[line_x(3), zd]
        if d:
            ps3[i] = value
            cp = remote(ps3.at[i], pr3.at[z], pzs.at[i], pzr.at[z], at(x, zd, c))
            cp.start()
            p_z.append(cp)
        else:
            quotient = value
    for d in (1, 7, 2, 6, 3, 5, 4):
        wait_recv(pr3.at[line_z(d)], pzr.at[line_z(d)])
        quotient = quotient + pr3[line_z(d)]

    previous = traces[...].astype(jnp.float32)
    for k in range(NB):
        before = previous[k : k + 1, :]
        grams = gcol[k]
        updated = jnp.maximum(before + quotient[k : k + 1, :] / grams[k : k + 1, :], 0.0)
        out[k : k + 1, :] = updated
        if k + 1 < NB:
            quotient = quotient - grams * (updated - before)

    for cp in t_z + t_x + [t_c, g_c] + g_x + g_z + p_c + p_x + p_z:
        cp.wait_send()

    @pl.when(x == y)
    def _():
        part_ = movie.at[pl.ds(0, 63)]
        remote(part_, part_, ms, ms, (t, y)).wait_send()

    @pl.when(x != y)
    def _():
        remote(movie, movie, ms, ms, (t, y)).wait_send()


def shards(movie_frames, footprints, tile_blocks, tile_count, traces):
    tiles_here, pixels, columns = footprints.shape
    tile_devices = lax.axis_size("tile")
    shard_rows = movie_frames.shape[0]
    movie = movie_frames.reshape(shard_rows, tile_devices, pixels // LANES, LANES)
    movie = movie.transpose(1, 2, 0, 3)
    f32, bf16 = jnp.float32, jnp.bfloat16
    dma = pltpu.SemaphoreType.DMA
    smem = pl.BlockSpec(memory_space=pltpu.SMEM)
    vmem = pl.BlockSpec(memory_space=pltpu.VMEM)
    hbm = pl.BlockSpec(memory_space=pl.ANY)
    tile = (NB, LANES)
    scratch = [
        pltpu.VMEM((pixels, columns), bf16),
        pltpu.VMEM((NZ, pixels // LANES, NC * NY, 2, LANES), bf16),
        pltpu.VMEM((LANES, pixels), f32),
        pltpu.VMEM((LANES, pixels), bf16),
        pltpu.VMEM((NX, NC, NZ) + tile, bf16),
        pltpu.VMEM((columns, LANES), f32),
        pltpu.VMEM((columns, columns), f32),
        pltpu.VMEM((SLOTS,) + tile, f32),
        pltpu.SMEM((64,), jnp.int32),
        pltpu.VMEM((SLOTS,) + tile, f32),
        pltpu.VMEM((NX,) + tile, f32),
        pltpu.VMEM((NX,) + tile, f32),
        pltpu.VMEM((3,) + tile, f32),
        pltpu.VMEM((NX,) + tile, f32),
        pltpu.VMEM(tile, f32),
        pltpu.VMEM((NZ,) + tile, f32),
        pltpu.VMEM((NB,) + tile, f32),
        pltpu.VMEM((NX, NZ) + tile, f32),
        pltpu.VMEM((NX, NZ) + tile, f32),
        pltpu.VMEM((NX, NZ) + tile, f32),
        pltpu.VMEM((NX, NZ) + tile, f32),
        pltpu.VMEM((7,) + tile, f32),
        pltpu.VMEM((NZ,) + tile, f32),
        dma, dma, dma((NZ,)),
        dma((7,)), dma((NZ,)), dma((3,)), dma((NX,)), dma, dma,
        dma, dma, dma((3,)), dma((NX,)), dma((7,)), dma((NZ,)),
        dma((NX,)), dma((NX,)), dma((3,)), dma((NX,)), dma((7,)), dma((NZ,)),
    ]
    return pl.pallas_call(
        kernel,
        out_shape=jax.ShapeDtypeStruct(tile, f32),
        in_specs=[smem, smem, hbm, hbm, vmem],
        out_specs=vmem,
        scratch_shapes=scratch,
        compiler_params=pltpu.CompilerParams(collective_id=1, has_side_effects=True),
        name="hals",
    )(tile_blocks, tile_count, movie, footprints.reshape(pixels, columns), traces)


def solution(mesh):
    placed = (
        P(("tile", "tm"), None),
        P("tile", None, None),
        P("tile", None),
        P("tile"),
        P("tile", "tm"),
    )
    return jax.shard_map(
        shards, mesh=mesh, in_specs=placed, out_specs=P("tile", "tm"), check_vma=False
    )
```

```python
import functools

import jax
import jax.numpy as jnp
from jax import lax
from jax.experimental import pallas as pl
from jax.experimental.pallas import tpu as pltpu
from jax.sharding import PartitionSpec as P

MESH = pl.DeviceIdType.MESH
NX, NY, NZ, NC = 4, 4, 8, 2
NB, SLOTS, LANES = 16, 16, 128
ROWS = NY * 2 * NC
FAR_FIRST = (4, 3, 5, 2, 6, 1, 7, 0)


def remote(src, dst, send, recv, device):
    return pltpu.make_async_remote_copy(
        src_ref=src, dst_ref=dst, send_sem=send, recv_sem=recv, device_id=device, device_id_type=MESH
    )


def kernel(
    blocks, count, blocks_hbm, count_hbm, movie, feet, traces, out,
    blocks_other, count_other, f_v, arrived, model, resid, products, table, chosen, gfull,
    inverse, part, part_other, grams, grams_other, gs2, gr2, gs3, gr3, gcol, ps2, pr2, ps3, pr3,
    near, f_sem, los, ms, mr, tzs, tzr, txs, txr, tcs, tcr,
    gcs, gcr, gxs, gxr, gzs, gzr, pcs, pcr, pxs, pxr, pzs, pzr,
):
    t = lax.axis_index("tile")
    y = lax.axis_index("tm")
    x = t // 16
    z = lax.rem(t // 2, 8)
    c = lax.rem(t, 2)
    pixels = f_v.shape[0]
    col_tiles = arrived.shape[1]

    def line_x(d):
        return lax.rem(x + d, NX)

    def line_z(d):
        return lax.rem(z + d, NZ)

    def at(x_, z_, c_):
        return (x_ * 16 + z_ * 2 + c_, y)

    f_copy = pltpu.make_async_copy(feet, f_v, f_sem)
    f_copy.start()

    barrier = pltpu.get_barrier_semaphore()

    def greet(device):
        pl.semaphore_signal(barrier, inc=1, device_id=device, device_id_type=MESH)

    for d in (1, 7):
        for r in range(8):
            greet((y * 16 + line_z(d) * 2 + r % 2, r // 2))
        greet(at(x, line_z(d), c))
    for r in range(8):
        source_tile = y * 16 + z * 2 + r % 2

        @pl.when(jnp.logical_or(source_tile != t, y != r // 2))
        def _():
            greet((source_tile, r // 2))

    for d in (2, 1, 3):
        greet(at(line_x(d), z, c))
    greet(at(x, z, 1 - c))
    pl.semaphore_wait(barrier, 30 - (x == y).astype(jnp.int32))

    known = [1, 1]
    below, above = at(x, line_z(7), c), at(x, line_z(1), c)

    def tell(way):
        pl.semaphore_signal(
            near.at[way], inc=1, device_id=(below, above)[way], device_id_type=MESH
        )

    def learn(way):
        pl.semaphore_wait(near.at[way], 1)
        known[way] += 1
        if known[way] < (4, 3)[way]:
            tell(way)

    tell(0)
    tell(1)

    lists = [
        remote(blocks_hbm, blocks_other, los.at[0], los.at[2], at(x, z, 1 - c)),
        remote(count_hbm, count_other, los.at[1], los.at[3], at(x, z, 1 - c)),
    ]
    for cp in lists:
        cp.start()

    landing = arrived.at[z, :, c * 4 + y]

    def send_movie(d):
        def body(r, carry):
            to = lax.rem(x + r // 2, NX) * 16 + line_z(d) * 2 + lax.rem(c + r, 2)
            if d:
                remote(movie.at[to], landing, ms, mr.at[z], (to, x)).start()
                return carry
            here = jnp.logical_and(to == t, x == y)

            @pl.when(jnp.logical_not(here))
            def _():
                remote(movie.at[to], landing, ms, mr.at[z], (to, x)).start()

            @pl.when(here)
            def _():
                pltpu.make_async_copy(movie.at[to], landing, mr.at[z]).start()

            return carry

        lax.fori_loop(0, 8, body, 0)

    table[x, c, z] = traces[...]
    t_z = []

    def send_traces(d):
        i = len(t_z)
        cp = remote(traces, table.at[x, c, z], tzs.at[i], tzr.at[z], at(x, line_z(d), c))
        cp.start()
        t_z.append(cp)

    def wait_recv(dst, sem):
        remote(dst, dst, sem, sem, (t, y)).wait_recv()

    send_traces(1)
    send_traces(7)
    send_movie(1)
    send_movie(7)
    send_movie(0)
    for way, d in ((0, 2), (1, 6), (0, 3), (1, 5), (0, 4)):
        learn(way)
        send_traces(d)
    for d in (4, 3, 5, 2, 6):
        send_movie(d)

    def find_all(row, blocks_, count_):
        place = []
        for s in range(SLOTS):
            b = blocks_[0, s]
            where_ = (b // 16) * 8 + lax.rem(b // 2, 8)
            mine = jnp.logical_and(s < count_[0], lax.rem(b, 2) == c)
            place.append(jnp.where(mine, where_, -1))

        def find(d, carry):
            found = jnp.int32(0)
            for s in range(SLOTS):
                found = found + jnp.where(place[s] == d, s + 1, 0)
            inverse[row, d] = found
            return carry

        lax.fori_loop(0, NX * NZ, find, 0)

    live_count = count[0]
    find_all(0, blocks, count)

    f_copy.wait()

    def gram_step(i, acc):
        rows = f_v[pl.ds(pl.multiple_of(i * 512, 512), 512), :]
        return acc + lax.dot_general(
            rows, rows, (((0,), (0,)), ((), ())), preferred_element_type=jnp.float32
        )

    gfull[...] = lax.fori_loop(
        0, pixels // 512, gram_step, jnp.zeros((SLOTS * NB, SLOTS * NB), jnp.float32)
    )
    lane = lax.broadcasted_iota(jnp.int32, (NB, LANES), 1)
    lane_block = lane // NB

    def spread(value):
        value = value + pltpu.roll(value, 16, 1)
        value = value + pltpu.roll(value, 32, 1)
        return value + pltpu.roll(value, 64, 1)

    row8 = lax.broadcasted_iota(jnp.int32, (8, LANES), 0)
    keep = row8 == lane_block[:8]
    for s in range(SLOTS):
        lanes = gfull[s * NB : (s + 1) * NB, (s // 8) * LANES : (s // 8 + 1) * LANES]
        wide = spread(jnp.where(lane_block == s % 8, lanes, 0.0))
        for half in range(2):
            grams[s, half : half + 1, :] = jnp.sum(
                jnp.where(keep, wide[half * 8 : half * 8 + 8, :], 0.0), axis=0, keepdims=True
            )
    g_c = remote(grams, grams_other, gcs, gcr, at(x, z, 1 - c))
    g_c.start()

    for d in range(1, NZ):
        wait_recv(table.at[x, c, line_z(d)], tzr.at[line_z(d)])
    t_x = []
    for i, d in enumerate((2, 1, 3)):
        cp = remote(table.at[x, c], table.at[x, c], txs.at[i], txr.at[x], at(line_x(d), z, c))
        cp.start()
        t_x.append(cp)

    wait_recv(blocks_other, los.at[2])
    wait_recv(count_other, los.at[3])
    find_all(1, blocks_other, count_other)

    def chip_sum(x_, z_, own, other):
        slot = inverse[0, x_ * 8 + z_]
        value = jnp.where(slot > 0, own[jnp.maximum(slot - 1, 0)], 0.0)
        slot = inverse[1, x_ * 8 + z_]
        return value + jnp.where(slot > 0, other[jnp.maximum(slot - 1, 0)], 0.0)

    g_c.wait_recv()
    g_x = []
    for i, d in enumerate((2, 1, 3, 0)):
        for z_ in range(NZ):
            gs2[i, z_] = chip_sum(line_x(d), z_, grams, grams_other)
        if d:
            cp = remote(gs2.at[i], gr2.at[x], gxs.at[i], gxr.at[x], at(line_x(d), z, c))
            cp.start()
            g_x.append(cp)

    for d in (2, 1, 3):
        wait_recv(table.at[line_x(d), c], txr.at[line_x(d)])
    t_c = remote(table.at[:, c], table.at[:, c], tcs, tcr, at(x, z, 1 - c))
    t_c.start()
    for d in (2, 1, 3):
        wait_recv(gr2.at[line_x(d)], gxr.at[line_x(d)])
    for z_ in range(NZ):
        gs3[z_] = gs2[3, z_] + gr2[line_x(1), z_] + gr2[line_x(2), z_] + gr2[line_x(3), z_]
    g_z = []
    for i, d in enumerate((4, 3, 5, 2, 6, 1, 7)):
        cp = remote(
            gs3.at[line_z(d)], gr3.at[z], gzs.at[i], gzr.at[z], at(x, line_z(d), c)
        )
        cp.start()
        g_z.append(cp)

    wait_recv(table.at[:, 1 - c], tcr)
    for s in range(SLOTS):
        b = blocks[0, s]
        value = table[b // 16, lax.rem(b, 2), lax.rem(b // 2, 8)]
        chosen[s * NB : (s + 1) * NB, :] = jnp.where(
            s < live_count, value.astype(jnp.float32), 0.0
        )
    picked = jnp.transpose(chosen[...]).astype(jnp.bfloat16)

    def model_step(i, carry):
        at_ = pl.ds(pl.multiple_of(i * 512, 512), 512)
        model[:, at_] = lax.dot_general(
            picked, f_v[at_, :], (((1,), (1,)), ((), ())), preferred_element_type=jnp.float32
        )
        return carry

    lax.fori_loop(0, pixels // 512, model_step, 0)

    for pair in ((1, 7), (0, 4), (3, 5), (2, 6)):
        for half, d in enumerate(pair):
            zs = lax.rem(z + NZ - d, NZ)
            wait_recv(arrived.at[zs], mr.at[zs])
            rows = pl.ds(pl.multiple_of(zs * ROWS, ROWS), ROWS)

            def residual_step(j, carry):
                for i in range(4):
                    col = pl.ds(pl.multiple_of(j * 512, 512) + i * LANES, LANES)
                    frames = arrived[zs, j * 4 + i].reshape(ROWS, LANES).astype(jnp.float32)
                    resid[half * ROWS : (half + 1) * ROWS, col] = (
                        frames - model[rows, col]
                    ).astype(jnp.bfloat16)
                return carry

            lax.fori_loop(0, col_tiles // 4, residual_step, 0)
        product = jnp.dot(resid[...], f_v[...], preferred_element_type=jnp.float32)
        for half, d in enumerate(pair):
            zs = lax.rem(z + NZ - d, NZ)
            rows = pl.ds(pl.multiple_of(zs * ROWS, ROWS), ROWS)
            products[rows, :] = product[half * ROWS : (half + 1) * ROWS, :]

    p_c, p_x, p_z = [], [], []
    for half in range(2):
        piece = pl.ds(half * 8, 8)
        part[piece] = jnp.transpose(
            products[:, half * LANES : (half + 1) * LANES]
        ).reshape(8, NB, LANES)
        cp = remote(
            part.at[piece], part_other.at[piece], pcs.at[half], pcr.at[half], at(x, z, 1 - c)
        )
        cp.start()
        p_c.append(cp)

    for d in range(1, NZ):
        wait_recv(gr3.at[line_z(d)], gzr.at[line_z(d)])
    packed = gs3[z]
    for d in range(1, NZ):
        packed = packed + gr3[line_z(d)]
    for half in range(2):
        wide = spread(
            jnp.where(keep, jnp.broadcast_to(packed[half : half + 1, :], (8, LANES)), 0.0)
        )
        for k in range(NB):
            column = jnp.sum(jnp.where(lane[:8] == k, wide, 0.0), axis=1, keepdims=True)
            gcol[k, half * 8 : half * 8 + 8, :] = jnp.broadcast_to(column, (8, LANES))

    for half in range(2):
        p_c[half].wait_recv()
    pieces = ((0, 1), (1, 3), (3, 5), (5, 8))
    for h, (lo, hi) in enumerate(pieces):
        for i, dx in enumerate((2, 1, 3)):
            xd = line_x(dx)
            for j in range(lo, hi):
                ps2[i, j] = chip_sum(xd, line_z(FAR_FIRST[j]), part, part_other)
            piece = pl.ds(lo, hi - lo)
            cp = remote(
                ps2.at[i, piece], pr2.at[x, piece], pxs.at[h, i], pxr.at[h, x], at(xd, z, c)
            )
            cp.start()
            p_x.append(cp)
    for j in range(NZ):
        ps2[3, j] = chip_sum(x, line_z(FAR_FIRST[j]), part, part_other)

    quotient = None
    for h, (lo, hi) in enumerate(pieces):
        for dx in (1, 3, 2):
            wait_recv(pr2.at[line_x(dx), pl.ds(lo, hi - lo)], pxr.at[h, line_x(dx)])
        for j in range(lo, hi):
            d = FAR_FIRST[j]
            value = ps2[3, j]
            for dx in (1, 2, 3):
                value = value + pr2[line_x(dx), j]
            if d:
                ps3[j] = value
                cp = remote(ps3.at[j], pr3.at[z], pzs.at[j], pzr.at[z], at(x, line_z(d), c))
                cp.start()
                p_z.append(cp)
            else:
                quotient = value
    for d in (1, 7, 2, 6, 3, 5, 4):
        wait_recv(pr3.at[line_z(d)], pzr.at[line_z(d)])
        quotient = quotient + pr3[line_z(d)]

    previous = traces[...].astype(jnp.float32)
    for k in range(NB):
        before = previous[k : k + 1, :]
        gram = gcol[k]
        updated = jnp.maximum(before + quotient[k : k + 1, :] / gram[k : k + 1, :], 0.0)
        out[k : k + 1, :] = updated
        if k + 1 < NB:
            quotient = quotient - gram * (updated - before)

    for cp in lists + t_z + t_x + [t_c, g_c] + g_x + g_z + p_c + p_x + p_z:
        cp.wait_send()

    @pl.when(x == y)
    def _():
        part_ = movie.at[pl.ds(0, 63)]
        remote(part_, part_, ms, ms, (t, y)).wait_send()

    @pl.when(x != y)
    def _():
        remote(movie, movie, ms, ms, (t, y)).wait_send()


def shards(movie_frames, footprints, tile_blocks, tile_count, traces):
    tiles_here, pixels, columns = footprints.shape
    tile_devices = lax.axis_size("tile")
    shard_rows = movie_frames.shape[0]
    movie = movie_frames.reshape(shard_rows, tile_devices, pixels // LANES, LANES)
    movie = movie.transpose(1, 2, 0, 3)
    f32, bf16 = jnp.float32, jnp.bfloat16
    dma = pltpu.SemaphoreType.DMA
    smem = pl.BlockSpec(memory_space=pltpu.SMEM)
    vmem = pl.BlockSpec(memory_space=pltpu.VMEM)
    hbm = pl.BlockSpec(memory_space=pl.ANY)
    tile = (NB, LANES)
    packed = (2, LANES)
    scratch = [
        pltpu.SMEM((1, SLOTS), jnp.int32),
        pltpu.SMEM((1,), jnp.int32),
        pltpu.VMEM((pixels, columns), bf16),
        pltpu.VMEM((NZ, pixels // LANES, NC * NY, 2, LANES), bf16),
        pltpu.VMEM((LANES, pixels), f32),
        pltpu.VMEM((2 * ROWS, pixels), bf16),
        pltpu.VMEM((LANES, columns), f32),
        pltpu.VMEM((NX, NC, NZ) + tile, bf16),
        pltpu.VMEM((columns, LANES), f32),
        pltpu.VMEM((columns, columns), f32),
        pltpu.SMEM((2, NX * NZ), jnp.int32),
        pltpu.VMEM((SLOTS,) + tile, f32),
        pltpu.VMEM((SLOTS,) + tile, f32),
        pltpu.VMEM((SLOTS,) + packed, f32),
        pltpu.VMEM((SLOTS,) + packed, f32),
        pltpu.VMEM((NX, NZ) + packed, f32),
        pltpu.VMEM((NX, NZ) + packed, f32),
        pltpu.VMEM((NZ,) + packed, f32),
        pltpu.VMEM((NZ,) + packed, f32),
        pltpu.VMEM((NB,) + tile, f32),
        pltpu.VMEM((NX, NZ) + tile, f32),
        pltpu.VMEM((NX, NZ) + tile, f32),
        pltpu.VMEM((7,) + tile, f32),
        pltpu.VMEM((NZ,) + tile, f32),
        pltpu.SemaphoreType.REGULAR((2,)), dma, dma((4,)), dma, dma((NZ,)),
        dma((7,)), dma((NZ,)), dma((3,)), dma((NX,)), dma, dma,
        dma, dma, dma((3,)), dma((NX,)), dma((7,)), dma((NZ,)),
        dma((2,)), dma((2,)), dma((4, 3)), dma((4, NX)), dma((7,)), dma((NZ,)),
    ]
    updated = pl.pallas_call(
        kernel,
        out_shape=jax.ShapeDtypeStruct(tile, f32),
        in_specs=[smem, smem, hbm, hbm, hbm, hbm, vmem],
        out_specs=vmem,
        scratch_shapes=scratch,
        compiler_params=pltpu.CompilerParams(collective_id=1, has_side_effects=True),
        name="hals",
    )(tile_blocks, tile_count, tile_blocks, tile_count, movie, footprints.reshape(pixels, columns), traces)
    return jnp.maximum(updated, 0.0)


def solution(mesh):
    placed = (
        P(("tile", "tm"), None),
        P("tile", None, None),
        P("tile", None),
        P("tile"),
        P("tile", "tm"),
    )
    return jax.shard_map(
        shards, mesh=mesh, in_specs=placed, out_specs=P("tile", "tm"), check_vma=False
    )
```

```python
import functools

import jax
import jax.numpy as jnp
from jax import lax
from jax.experimental import pallas as pl
from jax.experimental.pallas import tpu as pltpu
from jax.sharding import PartitionSpec as P

MESH = pl.DeviceIdType.MESH
NX, NY, NZ, NC = 4, 4, 8, 2
NB, SLOTS, LANES = 16, 16, 128
ROWS = NY * 2 * NC
FAR_FIRST = (4, 3, 5, 2, 6, 1, 7, 0)


def remote(src, dst, send, recv, device):
    return pltpu.make_async_remote_copy(
        src_ref=src, dst_ref=dst, send_sem=send, recv_sem=recv, device_id=device, device_id_type=MESH
    )


def kernel(
    blocks_hbm, count_hbm, movie, feet, traces, out,
    blocks, count, blocks_other, count_other, f_v, arrived, model, resid, products, table, chosen, gfull,
    inverse, part, part_other, grams, grams_other, gs2, gr2, gs3, gr3, gcol, ps2, pr2, ps3, pr3, pf1, pf2,
    near, f_sem, own, los, ms, mr, tzs, tzr, txs, txr, tcs, tcr,
    gcs, gcr, gxs, gxr, gzs, gzr, pcs, pcr, pxs, pxr, pzs, pzr, pfs, pfr,
):
    t = lax.axis_index("tile")
    y = lax.axis_index("tm")
    x = t // 16
    z = lax.rem(t // 2, 8)
    c = lax.rem(t, 2)
    pixels = f_v.shape[0]
    col_tiles = arrived.shape[1]

    def line_x(d):
        return lax.rem(x + d, NX)

    def line_z(d):
        return lax.rem(z + d, NZ)

    def at(x_, z_, c_):
        return (x_ * 16 + z_ * 2 + c_, y)

    f_copy = pltpu.make_async_copy(feet, f_v, f_sem)
    f_copy.start()
    own_copies = [
        pltpu.make_async_copy(blocks_hbm, blocks, own.at[0]),
        pltpu.make_async_copy(count_hbm, count, own.at[1]),
        pltpu.make_async_copy(traces, table.at[x, c, z], own.at[2]),
    ]
    for cp in own_copies:
        cp.start()

    barrier = pltpu.get_barrier_semaphore()

    def greet(device):
        pl.semaphore_signal(barrier, inc=1, device_id=device, device_id_type=MESH)

    for d in (1, 7):
        for r in range(8):
            greet((y * 16 + line_z(d) * 2 + r % 2, r // 2))
        greet(at(x, line_z(d), c))
    for r in range(8):
        source_tile = y * 16 + z * 2 + r % 2

        @pl.when(jnp.logical_or(source_tile != t, y != r // 2))
        def _():
            greet((source_tile, r // 2))

    for d in (2, 1, 3):
        greet(at(line_x(d), z, c))
    greet(at(x, z, 1 - c))
    pl.semaphore_wait(barrier, 30 - (x == y).astype(jnp.int32))

    known = [1, 1]
    below, above = at(x, line_z(7), c), at(x, line_z(1), c)

    def tell(way):
        pl.semaphore_signal(
            near.at[way], inc=1, device_id=(below, above)[way], device_id_type=MESH
        )

    def learn(way):
        pl.semaphore_wait(near.at[way], 1)
        known[way] += 1
        if known[way] < (4, 3)[way]:
            tell(way)

    tell(0)
    tell(1)

    lists = [
        remote(blocks_hbm, blocks_other, los.at[0], los.at[2], at(x, z, 1 - c)),
        remote(count_hbm, count_other, los.at[1], los.at[3], at(x, z, 1 - c)),
    ]
    for cp in lists:
        cp.start()

    landing = arrived.at[z, :, c * 4 + y]

    def send_movie(d):
        def body(r, carry):
            to = lax.rem(x + r // 2, NX) * 16 + line_z(d) * 2 + lax.rem(c + r, 2)
            if d:
                remote(movie.at[to], landing, ms, mr.at[z], (to, x)).start()
                return carry
            here = jnp.logical_and(to == t, x == y)

            @pl.when(jnp.logical_not(here))
            def _():
                remote(movie.at[to], landing, ms, mr.at[z], (to, x)).start()

            @pl.when(here)
            def _():
                pltpu.make_async_copy(movie.at[to], landing, mr.at[z]).start()

            return carry

        lax.fori_loop(0, 8, body, 0)

    t_z = []

    def send_traces(d):
        i = len(t_z)
        cp = remote(traces, table.at[x, c, z], tzs.at[i], tzr.at[z], at(x, line_z(d), c))
        cp.start()
        t_z.append(cp)

    def wait_recv(dst, sem):
        remote(dst, dst, sem, sem, (t, y)).wait_recv()

    send_traces(1)
    send_traces(7)
    send_movie(1)
    send_movie(7)
    send_movie(0)
    for way, d in ((0, 2), (1, 6), (0, 3), (1, 5), (0, 4)):
        learn(way)
        send_traces(d)
    for d in (4, 3, 5, 2, 6):
        send_movie(d)

    def find_all(row, blocks_, count_):
        place = []
        for s in range(SLOTS):
            b = blocks_[0, s]
            where_ = (b // 16) * 8 + lax.rem(b // 2, 8)
            mine = jnp.logical_and(s < count_[0], lax.rem(b, 2) == c)
            place.append(jnp.where(mine, where_, -1))

        def find(d, carry):
            found = jnp.int32(0)
            for s in range(SLOTS):
                found = found + jnp.where(place[s] == d, s + 1, 0)
            inverse[row, d] = found
            return carry

        lax.fori_loop(0, NX * NZ, find, 0)

    for cp in own_copies:
        cp.wait()
    live_count = count[0]
    find_all(0, blocks, count)

    f_copy.wait()

    def gram_step(i, acc):
        rows = f_v[pl.ds(pl.multiple_of(i * 512, 512), 512), :]
        return acc + lax.dot_general(
            rows, rows, (((0,), (0,)), ((), ())), preferred_element_type=jnp.float32
        )

    gfull[...] = lax.fori_loop(
        0, pixels // 512, gram_step, jnp.zeros((SLOTS * NB, SLOTS * NB), jnp.float32)
    )
    lane = lax.broadcasted_iota(jnp.int32, (NB, LANES), 1)
    lane_block = lane // NB

    def spread(value):
        value = value + pltpu.roll(value, 16, 1)
        value = value + pltpu.roll(value, 32, 1)
        return value + pltpu.roll(value, 64, 1)

    row8 = lax.broadcasted_iota(jnp.int32, (8, LANES), 0)
    keep = row8 == lane_block[:8]
    for s in range(SLOTS):
        lanes = gfull[s * NB : (s + 1) * NB, (s // 8) * LANES : (s // 8 + 1) * LANES]
        wide = spread(jnp.where(lane_block == s % 8, lanes, 0.0))
        for half in range(2):
            grams[s, half : half + 1, :] = jnp.sum(
                jnp.where(keep, wide[half * 8 : half * 8 + 8, :], 0.0), axis=0, keepdims=True
            )
    g_c = remote(grams, grams_other, gcs, gcr, at(x, z, 1 - c))
    g_c.start()

    for d in range(1, NZ):
        wait_recv(table.at[x, c, line_z(d)], tzr.at[line_z(d)])
    t_x = []
    for i, d in enumerate((2, 1, 3)):
        cp = remote(table.at[x, c], table.at[x, c], txs.at[i], txr.at[x], at(line_x(d), z, c))
        cp.start()
        t_x.append(cp)

    wait_recv(blocks_other, los.at[2])
    wait_recv(count_other, los.at[3])
    find_all(1, blocks_other, count_other)

    def chip_sum(x_, z_, own, other):
        slot = inverse[0, x_ * 8 + z_]
        value = jnp.where(slot > 0, own[jnp.maximum(slot - 1, 0)], 0.0)
        slot = inverse[1, x_ * 8 + z_]
        return value + jnp.where(slot > 0, other[jnp.maximum(slot - 1, 0)], 0.0)

    g_c.wait_recv()
    g_x = []
    for i, d in enumerate((2, 1, 3, 0)):
        for z_ in range(NZ):
            gs2[i, z_] = chip_sum(line_x(d), z_, grams, grams_other)
        if d:
            cp = remote(gs2.at[i], gr2.at[x], gxs.at[i], gxr.at[x], at(line_x(d), z, c))
            cp.start()
            g_x.append(cp)

    for d in (2, 1, 3):
        wait_recv(table.at[line_x(d), c], txr.at[line_x(d)])
    t_c = remote(table.at[:, c], table.at[:, c], tcs, tcr, at(x, z, 1 - c))
    t_c.start()
    for d in (2, 1, 3):
        wait_recv(gr2.at[line_x(d)], gxr.at[line_x(d)])
    for z_ in range(NZ):
        gs3[z_] = gs2[3, z_] + gr2[line_x(1), z_] + gr2[line_x(2), z_] + gr2[line_x(3), z_]
    g_z = []
    for i, d in enumerate((4, 3, 5, 2, 6, 1, 7)):
        cp = remote(
            gs3.at[line_z(d)], gr3.at[z], gzs.at[i], gzr.at[z], at(x, line_z(d), c)
        )
        cp.start()
        g_z.append(cp)

    wait_recv(table.at[:, 1 - c], tcr)
    for s in range(SLOTS):
        b = blocks[0, s]
        value = table[b // 16, lax.rem(b, 2), lax.rem(b // 2, 8)]
        chosen[s * NB : (s + 1) * NB, :] = jnp.where(
            s < live_count, value.astype(jnp.float32), 0.0
        )
    picked = jnp.transpose(chosen[...]).astype(jnp.bfloat16)

    def model_step(i, carry):
        at_ = pl.ds(pl.multiple_of(i * 512, 512), 512)
        model[:, at_] = lax.dot_general(
            picked, f_v[at_, :], (((1,), (1,)), ((), ())), preferred_element_type=jnp.float32
        )
        return carry

    lax.fori_loop(0, pixels // 512, model_step, 0)

    for pair in ((1, 7), (0, 4), (3, 5), (2, 6)):
        for half, d in enumerate(pair):
            zs = lax.rem(z + NZ - d, NZ)
            wait_recv(arrived.at[zs], mr.at[zs])
            rows = pl.ds(pl.multiple_of(zs * ROWS, ROWS), ROWS)

            def residual_step(j, carry):
                for i in range(4):
                    col = pl.ds(pl.multiple_of(j * 512, 512) + i * LANES, LANES)
                    frames = arrived[zs, j * 4 + i].reshape(ROWS, LANES).astype(jnp.float32)
                    resid[half * ROWS : (half + 1) * ROWS, col] = (
                        frames - model[rows, col]
                    ).astype(jnp.bfloat16)
                return carry

            lax.fori_loop(0, col_tiles // 4, residual_step, 0)
        product = jnp.dot(resid[...], f_v[...], preferred_element_type=jnp.float32)
        for half, d in enumerate(pair):
            zs = lax.rem(z + NZ - d, NZ)
            rows = pl.ds(pl.multiple_of(zs * ROWS, ROWS), ROWS)
            products[rows, :] = product[half * ROWS : (half + 1) * ROWS, :]

    p_c, p_x, p_z = [], [], []
    for half in range(2):
        piece = pl.ds(half * 8, 8)
        part[piece] = jnp.transpose(
            products[:, half * LANES : (half + 1) * LANES]
        ).reshape(8, NB, LANES)
        cp = remote(
            part.at[piece], part_other.at[piece], pcs.at[half], pcr.at[half], at(x, z, 1 - c)
        )
        cp.start()
        p_c.append(cp)

    for half in range(2):
        p_c[half].wait_recv()
    far, near_z = (4, 3, 5), (2, 6, 1, 7, 0)
    p_f = []

    def send_far(d):
        j = far.index(d)
        for i, dx in enumerate((2, 1, 3, 0)):
            xd = line_x(dx)
            pf1[j, i] = chip_sum(xd, line_z(d), part, part_other)
            cp = remote(
                pf1.at[j, i], pf2.at[j, x], pfs.at[j, i], pfr.at[j, x], at(xd, line_z(d), c)
            )
            cp.start()
            p_f.append(cp)

    pieces = ((0, 2), (2, 5))

    def send_piece(h):
        lo, hi = pieces[h]
        for i, dx in enumerate((2, 1, 3)):
            xd = line_x(dx)
            for j in range(lo, hi):
                ps2[i, j] = chip_sum(xd, line_z(near_z[j]), part, part_other)
            piece = pl.ds(lo, hi - lo)
            cp = remote(
                ps2.at[i, piece], pr2.at[x, piece], pxs.at[h, i], pxr.at[h, x], at(xd, z, c)
            )
            cp.start()
            p_x.append(cp)

    send_far(4)
    send_piece(0)
    send_far(3)
    send_far(5)
    send_piece(1)
    for j in range(5):
        ps2[3, j] = chip_sum(x, line_z(near_z[j]), part, part_other)

    quotient = None
    for h, (lo, hi) in enumerate(pieces):
        for dx in (1, 3, 2):
            wait_recv(pr2.at[line_x(dx), pl.ds(lo, hi - lo)], pxr.at[h, line_x(dx)])
        for j in range(lo, hi):
            d = near_z[j]
            value = ps2[3, j]
            for dx in (1, 2, 3):
                value = value + pr2[line_x(dx), j]
            if d:
                ps3[j] = value
                cp = remote(ps3.at[j], pr3.at[z], pzs.at[j], pzr.at[z], at(x, line_z(d), c))
                cp.start()
                p_z.append(cp)
            else:
                quotient = value

    for d in range(1, NZ):
        wait_recv(gr3.at[line_z(d)], gzr.at[line_z(d)])
    packed = gs3[z]
    for d in range(1, NZ):
        packed = packed + gr3[line_z(d)]
    for half in range(2):
        wide = spread(
            jnp.where(keep, jnp.broadcast_to(packed[half : half + 1, :], (8, LANES)), 0.0)
        )
        for k in range(NB):
            column = jnp.sum(jnp.where(lane[:8] == k, wide, 0.0), axis=1, keepdims=True)
            gcol[k, half * 8 : half * 8 + 8, :] = jnp.broadcast_to(column, (8, LANES))

    for d in (1, 7, 2, 6):
        wait_recv(pr3.at[line_z(d)], pzr.at[line_z(d)])
        quotient = quotient + pr3[line_z(d)]
    for j in (1, 2, 0):
        for dx in (0, 1, 3, 2):
            wait_recv(pf2.at[j, line_x(dx)], pfr.at[j, line_x(dx)])
            quotient = quotient + pf2[j, line_x(dx)]

    previous = table[x, c, z].astype(jnp.float32)
    for k in range(NB):
        before = previous[k : k + 1, :]
        gram = gcol[k]
        updated = jnp.maximum(before + quotient[k : k + 1, :] / gram[k : k + 1, :], 0.0)
        out[k : k + 1, :] = updated
        if k + 1 < NB:
            quotient = quotient - gram * (updated - before)

    for cp in lists + t_z + t_x + [t_c, g_c] + g_x + g_z + p_c + p_x + p_z + p_f:
        cp.wait_send()

    @pl.when(x == y)
    def _():
        part_ = movie.at[pl.ds(0, 63)]
        remote(part_, part_, ms, ms, (t, y)).wait_send()

    @pl.when(x != y)
    def _():
        remote(movie, movie, ms, ms, (t, y)).wait_send()


def shards(movie_frames, footprints, tile_blocks, tile_count, traces):
    tiles_here, pixels, columns = footprints.shape
    tile_devices = lax.axis_size("tile")
    shard_rows = movie_frames.shape[0]
    movie = movie_frames.reshape(shard_rows, tile_devices, pixels // LANES, LANES)
    movie = movie.transpose(1, 2, 0, 3)
    f32, bf16 = jnp.float32, jnp.bfloat16
    dma = pltpu.SemaphoreType.DMA
    vmem = pl.BlockSpec(memory_space=pltpu.VMEM)
    hbm = pl.BlockSpec(memory_space=pl.ANY)
    tile = (NB, LANES)
    packed = (2, LANES)
    scratch = [
        pltpu.SMEM((1, SLOTS), jnp.int32),
        pltpu.SMEM((1,), jnp.int32),
        pltpu.SMEM((1, SLOTS), jnp.int32),
        pltpu.SMEM((1,), jnp.int32),
        pltpu.VMEM((pixels, columns), bf16),
        pltpu.VMEM((NZ, pixels // LANES, NC * NY, 2, LANES), bf16),
        pltpu.VMEM((LANES, pixels), f32),
        pltpu.VMEM((2 * ROWS, pixels), bf16),
        pltpu.VMEM((LANES, columns), f32),
        pltpu.VMEM((NX, NC, NZ) + tile, bf16),
        pltpu.VMEM((columns, LANES), f32),
        pltpu.VMEM((columns, columns), f32),
        pltpu.SMEM((2, NX * NZ), jnp.int32),
        pltpu.VMEM((SLOTS,) + tile, f32),
        pltpu.VMEM((SLOTS,) + tile, f32),
        pltpu.VMEM((SLOTS,) + packed, f32),
        pltpu.VMEM((SLOTS,) + packed, f32),
        pltpu.VMEM((NX, NZ) + packed, f32),
        pltpu.VMEM((NX, NZ) + packed, f32),
        pltpu.VMEM((NZ,) + packed, f32),
        pltpu.VMEM((NZ,) + packed, f32),
        pltpu.VMEM((NB,) + tile, f32),
        pltpu.VMEM((NX, 5) + tile, f32),
        pltpu.VMEM((NX, 5) + tile, f32),
        pltpu.VMEM((4,) + tile, f32),
        pltpu.VMEM((NZ,) + tile, f32),
        pltpu.VMEM((3, NX) + tile, f32),
        pltpu.VMEM((3, NX) + tile, f32),
        pltpu.SemaphoreType.REGULAR((2,)), dma, dma((3,)), dma((4,)), dma, dma((NZ,)),
        dma((7,)), dma((NZ,)), dma((3,)), dma((NX,)), dma, dma,
        dma, dma, dma((3,)), dma((NX,)), dma((7,)), dma((NZ,)),
        dma((2,)), dma((2,)), dma((2, 3)), dma((2, NX)), dma((4,)), dma((NZ,)),
        dma((3, NX)), dma((3, NX)),
    ]
    updated = pl.pallas_call(
        kernel,
        out_shape=pltpu.VMEM(tile, f32),
        in_specs=[hbm] * 5,
        out_specs=vmem,
        scratch_shapes=scratch,
        compiler_params=pltpu.CompilerParams(collective_id=1, has_side_effects=True),
        name="hals",
    )(tile_blocks, tile_count, movie, footprints.reshape(pixels, columns), traces)
    return jnp.maximum(updated, 0.0)


def solution(mesh):
    placed = (
        P(("tile", "tm"), None),
        P("tile", None, None),
        P("tile", None),
        P("tile"),
        P("tile", "tm"),
    )
    return jax.shard_map(
        shards, mesh=mesh, in_specs=placed, out_specs=P("tile", "tm"), check_vma=False
    )
```

```python
import functools

import jax
import jax.numpy as jnp
from jax import lax
from jax.experimental import pallas as pl
from jax.experimental.pallas import tpu as pltpu
from jax.sharding import PartitionSpec as P

MESH = pl.DeviceIdType.MESH
NX, NY, NZ, NC = 4, 4, 8, 2
NB, SLOTS, LANES = 16, 16, 128
ROWS = NY * 2 * NC
FAR_FIRST = (4, 3, 5, 2, 6, 1, 7, 0)


def remote(src, dst, send, recv, device):
    return pltpu.make_async_remote_copy(
        src_ref=src, dst_ref=dst, send_sem=send, recv_sem=recv, device_id=device, device_id_type=MESH
    )


def kernel(
    blocks_hbm, count_hbm, movie, feet, traces, out,
    blocks, count, blocks_other, count_other, f_v, arrived, model, products, table, chosen, gfull,
    inverse, part, part_other, grams, grams_other, gs2, gr2, gs3, gr3, gcol, ps2, pr2, ps3, pr3, pf1, pf2,
    near, f_sem, own, los, ms, mr, tzs, tzr, txs, txr, tcs, tcr,
    gcs, gcr, gxs, gxr, gzs, gzr, pcs, pcr, pxs, pxr, pzs, pzr, pfs, pfr,
):
    t = lax.axis_index("tile")
    y = lax.axis_index("tm")
    x = t // 16
    z = lax.rem(t // 2, 8)
    c = lax.rem(t, 2)
    pixels = f_v.shape[0]

    def line_x(d):
        return lax.rem(x + d, NX)

    def line_z(d):
        return lax.rem(z + d, NZ)

    def at(x_, z_, c_):
        return (x_ * 16 + z_ * 2 + c_, y)

    f_copy = pltpu.make_async_copy(feet, f_v, f_sem)
    f_copy.start()
    own_copies = [
        pltpu.make_async_copy(blocks_hbm, blocks, own.at[0]),
        pltpu.make_async_copy(count_hbm, count, own.at[1]),
        pltpu.make_async_copy(traces, table.at[x, c, z], own.at[2]),
    ]
    for cp in own_copies:
        cp.start()

    barrier = pltpu.get_barrier_semaphore()

    def greet(device):
        pl.semaphore_signal(barrier, inc=1, device_id=device, device_id_type=MESH)

    for d in (1, 7):
        for r in range(8):
            greet((y * 16 + line_z(d) * 2 + r % 2, r // 2))
        greet(at(x, line_z(d), c))
    for r in range(8):
        source_tile = y * 16 + z * 2 + r % 2

        @pl.when(jnp.logical_or(source_tile != t, y != r // 2))
        def _():
            greet((source_tile, r // 2))

    for d in (2, 1, 3):
        greet(at(line_x(d), z, c))
    greet(at(x, z, 1 - c))
    pl.semaphore_wait(barrier, 30 - (x == y).astype(jnp.int32))

    known = [1, 1]
    below, above = at(x, line_z(7), c), at(x, line_z(1), c)

    def tell(way):
        pl.semaphore_signal(
            near.at[way], inc=1, device_id=(below, above)[way], device_id_type=MESH
        )

    def learn(way):
        pl.semaphore_wait(near.at[way], 1)
        known[way] += 1
        if known[way] < (4, 3)[way]:
            tell(way)

    tell(0)
    tell(1)

    lists = [
        remote(blocks_hbm, blocks_other, los.at[0], los.at[2], at(x, z, 1 - c)),
        remote(count_hbm, count_other, los.at[1], los.at[3], at(x, z, 1 - c)),
    ]
    for cp in lists:
        cp.start()

    landing = arrived.at[z, :, c * 4 + y]

    def send_movie(d):
        def body(r, carry):
            to = lax.rem(x + r // 2, NX) * 16 + line_z(d) * 2 + lax.rem(c + r, 2)
            if d:
                remote(movie.at[to], landing, ms, mr.at[z], (to, x)).start()
                return carry
            here = jnp.logical_and(to == t, x == y)

            @pl.when(jnp.logical_not(here))
            def _():
                remote(movie.at[to], landing, ms, mr.at[z], (to, x)).start()

            @pl.when(here)
            def _():
                pltpu.make_async_copy(movie.at[to], landing, mr.at[z]).start()

            return carry

        lax.fori_loop(0, 8, body, 0)

    t_z = []

    def send_traces(d):
        i = len(t_z)
        cp = remote(traces, table.at[x, c, z], tzs.at[i], tzr.at[z], at(x, line_z(d), c))
        cp.start()
        t_z.append(cp)

    def wait_recv(dst, sem):
        remote(dst, dst, sem, sem, (t, y)).wait_recv()

    send_traces(1)
    send_traces(7)
    send_movie(1)
    send_movie(7)
    send_movie(0)
    for way, d in ((0, 2), (1, 6), (0, 3), (1, 5), (0, 4)):
        learn(way)
        send_traces(d)
    for d in (4, 3, 5, 2, 6):
        send_movie(d)

    def find_all(row, blocks_, count_):
        place = []
        for s in range(SLOTS):
            b = blocks_[0, s]
            where_ = (b // 16) * 8 + lax.rem(b // 2, 8)
            mine = jnp.logical_and(s < count_[0, 0], lax.rem(b, 2) == c)
            place.append(jnp.where(mine, where_, -1))

        def find(d, carry):
            found = jnp.int32(0)
            for s in range(SLOTS):
                found = found + jnp.where(place[s] == d, s + 1, 0)
            inverse[row, d] = found
            return carry

        lax.fori_loop(0, NX * NZ, find, 0)

    for cp in own_copies:
        cp.wait()
    live_count = count[0, 0]
    find_all(0, blocks, count)

    f_copy.wait()

    def gram_step(i, acc):
        rows = f_v[pl.ds(pl.multiple_of(i * 512, 512), 512), :]
        return acc + lax.dot_general(
            rows, rows, (((0,), (0,)), ((), ())), preferred_element_type=jnp.float32
        )

    gfull[...] = lax.fori_loop(
        0, pixels // 512, gram_step, jnp.zeros((SLOTS * NB, SLOTS * NB), jnp.float32)
    )
    lane = lax.broadcasted_iota(jnp.int32, (NB, LANES), 1)
    lane_block = lane // NB

    def spread(value):
        value = value + pltpu.roll(value, 16, 1)
        value = value + pltpu.roll(value, 32, 1)
        return value + pltpu.roll(value, 64, 1)

    row8 = lax.broadcasted_iota(jnp.int32, (8, LANES), 0)
    keep = row8 == lane_block[:8]
    for s in range(SLOTS):
        lanes = gfull[s * NB : (s + 1) * NB, (s // 8) * LANES : (s // 8 + 1) * LANES]
        wide = spread(jnp.where(lane_block == s % 8, lanes, 0.0))
        for half in range(2):
            grams[s, half : half + 1, :] = jnp.sum(
                jnp.where(keep, wide[half * 8 : half * 8 + 8, :], 0.0), axis=0, keepdims=True
            )
    g_c = remote(grams, grams_other, gcs, gcr, at(x, z, 1 - c))
    g_c.start()

    for d in range(1, NZ):
        wait_recv(table.at[x, c, line_z(d)], tzr.at[line_z(d)])
    t_x = []
    for i, d in enumerate((2, 1, 3)):
        cp = remote(table.at[x, c], table.at[x, c], txs.at[i], txr.at[x], at(line_x(d), z, c))
        cp.start()
        t_x.append(cp)

    wait_recv(blocks_other, los.at[2])
    wait_recv(count_other, los.at[3])
    find_all(1, blocks_other, count_other)

    def chip_sum(x_, z_, own, other):
        slot = inverse[0, x_ * 8 + z_]
        value = jnp.where(slot > 0, own[jnp.maximum(slot - 1, 0)], 0.0)
        slot = inverse[1, x_ * 8 + z_]
        return value + jnp.where(slot > 0, other[jnp.maximum(slot - 1, 0)], 0.0)

    g_c.wait_recv()
    g_x = []
    for i, d in enumerate((2, 1, 3, 0)):
        for z_ in range(NZ):
            gs2[i, z_] = chip_sum(line_x(d), z_, grams, grams_other)
        if d:
            cp = remote(gs2.at[i], gr2.at[x], gxs.at[i], gxr.at[x], at(line_x(d), z, c))
            cp.start()
            g_x.append(cp)

    for d in (2, 1, 3):
        wait_recv(table.at[line_x(d), c], txr.at[line_x(d)])
    t_c = remote(table.at[:, c], table.at[:, c], tcs, tcr, at(x, z, 1 - c))
    t_c.start()
    for d in (2, 1, 3):
        wait_recv(gr2.at[line_x(d)], gxr.at[line_x(d)])
    for z_ in range(NZ):
        gs3[z_] = gs2[3, z_] + gr2[line_x(1), z_] + gr2[line_x(2), z_] + gr2[line_x(3), z_]
    g_z = []
    for i, d in enumerate((4, 3, 5, 2, 6, 1, 7)):
        cp = remote(
            gs3.at[line_z(d)], gr3.at[z], gzs.at[i], gzr.at[z], at(x, line_z(d), c)
        )
        cp.start()
        g_z.append(cp)

    wait_recv(table.at[:, 1 - c], tcr)
    for s in range(SLOTS):
        b = blocks[0, s]
        value = table[b // 16, lax.rem(b, 2), lax.rem(b // 2, 8)]
        chosen[s * NB : (s + 1) * NB, :] = jnp.where(
            s < live_count, value.astype(jnp.float32), 0.0
        )
    picked = jnp.transpose(chosen[...]).astype(jnp.bfloat16)

    def model_step(i, carry):
        at_ = pl.ds(pl.multiple_of(i * 512, 512), 512)
        model[:, at_] = lax.dot_general(
            picked, f_v[at_, :], (((1,), (1,)), ((), ())), preferred_element_type=jnp.float32
        )
        return carry

    lax.fori_loop(0, pixels // 512, model_step, 0)

    for pair in ((1, 7), (0, 4), (3, 5), (2, 6)):
        sources = [lax.rem(z + NZ - d, NZ) for d in pair]
        rows = [pl.ds(pl.multiple_of(zs * ROWS, ROWS), ROWS) for zs in sources]
        for zs in sources:
            wait_recv(arrived.at[zs], mr.at[zs])

        def product_step(j, acc):
            pieces = []
            for i in range(8):
                col = pl.ds(pl.multiple_of(j * 1024, 1024) + i * LANES, LANES)
                halves = []
                for half in range(2):
                    frames = arrived[sources[half], j * 8 + i].reshape(ROWS, LANES)
                    halves.append(frames.astype(jnp.float32) - model[rows[half], col])
                pieces.append(jnp.concatenate(halves, axis=0).astype(jnp.bfloat16))
            residual = jnp.concatenate(pieces, axis=1)
            at_ = pl.ds(pl.multiple_of(j * 1024, 1024), 1024)
            return acc + jnp.dot(residual, f_v[at_, :], preferred_element_type=jnp.float32)

        product = lax.fori_loop(
            0, pixels // 1024, product_step, jnp.zeros((2 * ROWS, SLOTS * NB), jnp.float32),
            unroll=True,
        )
        for half in range(2):
            products[rows[half], :] = product[half * ROWS : (half + 1) * ROWS, :]

    p_c, p_x, p_z = [], [], []
    for half in range(2):
        piece = pl.ds(half * 8, 8)
        part[piece] = jnp.transpose(
            products[:, half * LANES : (half + 1) * LANES]
        ).reshape(8, NB, LANES)
        cp = remote(
            part.at[piece], part_other.at[piece], pcs.at[half], pcr.at[half], at(x, z, 1 - c)
        )
        cp.start()
        p_c.append(cp)

    for half in range(2):
        p_c[half].wait_recv()
    far, near_z = (4, 3, 5), (2, 6, 1, 7, 0)
    p_f = []

    def send_far(d):
        j = far.index(d)
        for i, dx in enumerate((2, 1, 3, 0)):
            xd = line_x(dx)
            pf1[j, i] = chip_sum(xd, line_z(d), part, part_other)
            cp = remote(
                pf1.at[j, i], pf2.at[j, x], pfs.at[j, i], pfr.at[j, x], at(xd, line_z(d), c)
            )
            cp.start()
            p_f.append(cp)

    pieces = ((0, 2), (2, 5))

    def send_piece(h):
        lo, hi = pieces[h]
        for i, dx in enumerate((2, 1, 3)):
            xd = line_x(dx)
            for j in range(lo, hi):
                ps2[i, j] = chip_sum(xd, line_z(near_z[j]), part, part_other)
            piece = pl.ds(lo, hi - lo)
            cp = remote(
                ps2.at[i, piece], pr2.at[x, piece], pxs.at[h, i], pxr.at[h, x], at(xd, z, c)
            )
            cp.start()
            p_x.append(cp)

    send_far(4)
    send_piece(0)
    send_far(3)
    send_far(5)
    send_piece(1)
    for j in range(5):
        ps2[3, j] = chip_sum(x, line_z(near_z[j]), part, part_other)

    quotient = None
    for h, (lo, hi) in enumerate(pieces):
        for dx in (1, 3, 2):
            wait_recv(pr2.at[line_x(dx), pl.ds(lo, hi - lo)], pxr.at[h, line_x(dx)])
        for j in range(lo, hi):
            d = near_z[j]
            value = ps2[3, j]
            for dx in (1, 2, 3):
                value = value + pr2[line_x(dx), j]
            if d:
                ps3[j] = value
                cp = remote(ps3.at[j], pr3.at[z], pzs.at[j], pzr.at[z], at(x, line_z(d), c))
                cp.start()
                p_z.append(cp)
            else:
                quotient = value

    for d in range(1, NZ):
        wait_recv(gr3.at[line_z(d)], gzr.at[line_z(d)])
    packed = gs3[z]
    for d in range(1, NZ):
        packed = packed + gr3[line_z(d)]
    for half in range(2):
        wide = spread(
            jnp.where(keep, jnp.broadcast_to(packed[half : half + 1, :], (8, LANES)), 0.0)
        )
        for k in range(NB):
            column = jnp.sum(jnp.where(lane[:8] == k, wide, 0.0), axis=1, keepdims=True)
            gcol[k, half * 8 : half * 8 + 8, :] = jnp.broadcast_to(column, (8, LANES))

    for d in (1, 7, 2, 6):
        wait_recv(pr3.at[line_z(d)], pzr.at[line_z(d)])
        quotient = quotient + pr3[line_z(d)]
    for j in (1, 2, 0):
        for dx in (0, 1, 3, 2):
            wait_recv(pf2.at[j, line_x(dx)], pfr.at[j, line_x(dx)])
            quotient = quotient + pf2[j, line_x(dx)]

    previous = table[x, c, z].astype(jnp.float32)
    for k in range(NB):
        before = previous[k : k + 1, :]
        gram = gcol[k]
        updated = jnp.maximum(before + quotient[k : k + 1, :] / gram[k : k + 1, :], 0.0)
        out[k : k + 1, :] = updated
        if k + 1 < NB:
            quotient = quotient - gram * (updated - before)

    for cp in lists + t_z + t_x + [t_c, g_c] + g_x + g_z + p_c + p_x + p_z + p_f:
        cp.wait_send()

    @pl.when(x == y)
    def _():
        part_ = movie.at[pl.ds(0, 63)]
        remote(part_, part_, ms, ms, (t, y)).wait_send()

    @pl.when(x != y)
    def _():
        remote(movie, movie, ms, ms, (t, y)).wait_send()


def shards(movie_frames, footprints, tile_blocks, tile_count, traces):
    tiles_here, pixels, columns = footprints.shape
    tile_devices = lax.axis_size("tile")
    shard_rows = movie_frames.shape[0]
    movie = movie_frames.reshape(shard_rows, tile_devices, pixels // LANES, LANES)
    movie = movie.transpose(1, 2, 0, 3)
    f32, bf16 = jnp.float32, jnp.bfloat16
    dma = pltpu.SemaphoreType.DMA
    vmem = pl.BlockSpec(memory_space=pltpu.VMEM)
    hbm = pl.BlockSpec(memory_space=pl.ANY)
    tile = (NB, LANES)
    packed = (2, LANES)
    scratch = [
        pltpu.SMEM((1, SLOTS), jnp.int32),
        pltpu.SMEM((1, 1), jnp.int32),
        pltpu.SMEM((1, SLOTS), jnp.int32),
        pltpu.SMEM((1, 1), jnp.int32),
        pltpu.VMEM((pixels, columns), bf16),
        pltpu.VMEM((NZ, pixels // LANES, NC * NY, 2, LANES), bf16),
        pltpu.VMEM((LANES, pixels), f32),
        pltpu.VMEM((LANES, columns), f32),
        pltpu.VMEM((NX, NC, NZ) + tile, bf16),
        pltpu.VMEM((columns, LANES), f32),
        pltpu.VMEM((columns, columns), f32),
        pltpu.SMEM((2, NX * NZ), jnp.int32),
        pltpu.VMEM((SLOTS,) + tile, f32),
        pltpu.VMEM((SLOTS,) + tile, f32),
        pltpu.VMEM((SLOTS,) + packed, f32),
        pltpu.VMEM((SLOTS,) + packed, f32),
        pltpu.VMEM((NX, NZ) + packed, f32),
        pltpu.VMEM((NX, NZ) + packed, f32),
        pltpu.VMEM((NZ,) + packed, f32),
        pltpu.VMEM((NZ,) + packed, f32),
        pltpu.VMEM((NB,) + tile, f32),
        pltpu.VMEM((NX, 5) + tile, f32),
        pltpu.VMEM((NX, 5) + tile, f32),
        pltpu.VMEM((4,) + tile, f32),
        pltpu.VMEM((NZ,) + tile, f32),
        pltpu.VMEM((3, NX) + tile, f32),
        pltpu.VMEM((3, NX) + tile, f32),
        pltpu.SemaphoreType.REGULAR((2,)), dma, dma((3,)), dma((4,)), dma, dma((NZ,)),
        dma((7,)), dma((NZ,)), dma((3,)), dma((NX,)), dma, dma,
        dma, dma, dma((3,)), dma((NX,)), dma((7,)), dma((NZ,)),
        dma((2,)), dma((2,)), dma((2, 3)), dma((2, NX)), dma((4,)), dma((NZ,)),
        dma((3, NX)), dma((3, NX)),
    ]
    updated = pl.pallas_call(
        kernel,
        out_shape=pltpu.VMEM(tile, f32),
        in_specs=[hbm] * 5,
        out_specs=vmem,
        scratch_shapes=scratch,
        compiler_params=pltpu.CompilerParams(collective_id=1, has_side_effects=True),
        name="hals",
    )(tile_blocks, tile_count.reshape(1, 1), movie, footprints.reshape(pixels, columns), traces)
    return jnp.maximum(updated, 0.0)


def solution(mesh):
    placed = (
        P(("tile", "tm"), None),
        P("tile", None, None),
        P("tile", None),
        P("tile"),
        P("tile", "tm"),
    )
    return jax.shard_map(
        shards, mesh=mesh, in_specs=placed, out_specs=P("tile", "tm"), check_vma=False
    )
```

```python
import functools

import jax
import jax.numpy as jnp
from jax import lax
from jax.experimental import pallas as pl
from jax.experimental.pallas import tpu as pltpu
from jax.sharding import PartitionSpec as P

MESH = pl.DeviceIdType.MESH
NX, NY, NZ, NC = 4, 4, 8, 2
NB, SLOTS, LANES = 16, 16, 128
ROWS = NY * 2 * NC
FAR_FIRST = (4, 3, 5, 2, 6, 1, 7, 0)


def remote(src, dst, send, recv, device):
    return pltpu.make_async_remote_copy(
        src_ref=src, dst_ref=dst, send_sem=send, recv_sem=recv, device_id=device, device_id_type=MESH
    )


def kernel(
    blocks_hbm, count_hbm, movie, feet, traces, out,
    blocks, count, blocks_other, count_other, f_v, arrived, model, products, table, chosen, gfull,
    inverse, part, part_other, grams, grams_other, gs2, gr2, gs3, gr3, gcol, ps2, pr2, ps3, pr3, pf1, pf2,
    near, f_sem, own, los, ms, mr, tzs, tzr, txs, txr, tcs, tcr,
    gcs, gcr, gxs, gxr, gzs, gzr, pcs, pcr, pxs, pxr, pzs, pzr, pfs, pfr,
):
    t = lax.axis_index("tile")
    y = lax.axis_index("tm")
    x = t // 16
    z = lax.rem(t // 2, 8)
    c = lax.rem(t, 2)
    pixels = f_v.shape[0]

    def line_x(d):
        return lax.rem(x + d, NX)

    def line_z(d):
        return lax.rem(z + d, NZ)

    def at(x_, z_, c_):
        return (x_ * 16 + z_ * 2 + c_, y)

    f_copy = pltpu.make_async_copy(feet, f_v, f_sem)
    f_copy.start()
    own_copies = [
        pltpu.make_async_copy(blocks_hbm, blocks, own.at[0]),
        pltpu.make_async_copy(count_hbm, count, own.at[1]),
        pltpu.make_async_copy(traces, table.at[x, c, z], own.at[2]),
    ]
    for cp in own_copies:
        cp.start()

    barrier = pltpu.get_barrier_semaphore()

    def greet(device):
        pl.semaphore_signal(barrier, inc=1, device_id=device, device_id_type=MESH)

    for d in (1, 7):
        for r in range(8):
            greet((y * 16 + line_z(d) * 2 + r % 2, r // 2))
        greet(at(x, line_z(d), c))
    for r in range(8):
        source_tile = y * 16 + z * 2 + r % 2

        @pl.when(jnp.logical_or(source_tile != t, y != r // 2))
        def _():
            greet((source_tile, r // 2))

    for d in (2, 1, 3):
        greet(at(line_x(d), z, c))
    greet(at(x, z, 1 - c))
    pl.semaphore_wait(barrier, 30 - (x == y).astype(jnp.int32))

    known = [1, 1]
    below, above = at(x, line_z(7), c), at(x, line_z(1), c)

    def tell(way):
        pl.semaphore_signal(
            near.at[way], inc=1, device_id=(below, above)[way], device_id_type=MESH
        )

    def learn(way):
        pl.semaphore_wait(near.at[way], 1)
        known[way] += 1
        if known[way] < (4, 3)[way]:
            tell(way)

    tell(0)
    tell(1)

    lists = [
        remote(blocks_hbm, blocks_other, los.at[0], los.at[2], at(x, z, 1 - c)),
        remote(count_hbm, count_other, los.at[1], los.at[3], at(x, z, 1 - c)),
    ]
    for cp in lists:
        cp.start()

    landing = arrived.at[z, :, c * 4 + y]

    def send_movie(d):
        def body(r, carry):
            to = lax.rem(x + r // 2, NX) * 16 + line_z(d) * 2 + lax.rem(c + r, 2)
            if d:
                remote(movie.at[to], landing, ms, mr.at[z], (to, x)).start()
                return carry
            here = jnp.logical_and(to == t, x == y)

            @pl.when(jnp.logical_not(here))
            def _():
                remote(movie.at[to], landing, ms, mr.at[z], (to, x)).start()

            @pl.when(here)
            def _():
                pltpu.make_async_copy(movie.at[to], landing, mr.at[z]).start()

            return carry

        lax.fori_loop(0, 8, body, 0)

    t_z = []

    def send_traces(d):
        i = len(t_z)
        cp = remote(traces, table.at[x, c, z], tzs.at[i], tzr.at[z], at(x, line_z(d), c))
        cp.start()
        t_z.append(cp)

    def wait_recv(dst, sem):
        remote(dst, dst, sem, sem, (t, y)).wait_recv()

    send_traces(1)
    send_traces(7)
    send_movie(1)
    send_movie(7)
    send_movie(0)
    for way, d in ((0, 2), (1, 6), (0, 3), (1, 5), (0, 4)):
        learn(way)
        send_traces(d)
    for d in (3, 5, 4, 2, 6):
        send_movie(d)

    def find_all(row, blocks_, count_):
        place = []
        for s in range(SLOTS):
            b = blocks_[0, s]
            where_ = (b // 16) * 8 + lax.rem(b // 2, 8)
            mine = jnp.logical_and(s < count_[0, 0], lax.rem(b, 2) == c)
            place.append(jnp.where(mine, where_, -1))

        def find(d, carry):
            found = jnp.int32(0)
            for s in range(SLOTS):
                found = found + jnp.where(place[s] == d, s + 1, 0)
            inverse[row, d] = found
            return carry

        lax.fori_loop(0, NX * NZ, find, 0)

    for cp in own_copies:
        cp.wait()
    live_count = count[0, 0]
    find_all(0, blocks, count)

    f_copy.wait()

    def gram_step(i, acc):
        rows = f_v[pl.ds(pl.multiple_of(i * 512, 512), 512), :]
        return acc + lax.dot_general(
            rows, rows, (((0,), (0,)), ((), ())), preferred_element_type=jnp.float32
        )

    gfull[...] = lax.fori_loop(
        0, pixels // 512, gram_step, jnp.zeros((SLOTS * NB, SLOTS * NB), jnp.float32)
    )
    lane = lax.broadcasted_iota(jnp.int32, (NB, LANES), 1)
    lane_block = lane // NB

    def spread(value):
        value = value + pltpu.roll(value, 16, 1)
        value = value + pltpu.roll(value, 32, 1)
        return value + pltpu.roll(value, 64, 1)

    row8 = lax.broadcasted_iota(jnp.int32, (8, LANES), 0)
    keep = row8 == lane_block[:8]
    for s in range(SLOTS):
        lanes = gfull[s * NB : (s + 1) * NB, (s // 8) * LANES : (s // 8 + 1) * LANES]
        wide = spread(jnp.where(lane_block == s % 8, lanes, 0.0))
        for half in range(2):
            grams[s, half : half + 1, :] = jnp.sum(
                jnp.where(keep, wide[half * 8 : half * 8 + 8, :], 0.0), axis=0, keepdims=True
            )
    g_c = remote(grams, grams_other, gcs, gcr, at(x, z, 1 - c))
    g_c.start()

    for d in range(1, NZ):
        wait_recv(table.at[x, c, line_z(d)], tzr.at[line_z(d)])
    t_x = []
    for i, d in enumerate((2, 1, 3)):
        cp = remote(table.at[x, c], table.at[x, c], txs.at[i], txr.at[x], at(line_x(d), z, c))
        cp.start()
        t_x.append(cp)

    wait_recv(blocks_other, los.at[2])
    wait_recv(count_other, los.at[3])
    find_all(1, blocks_other, count_other)

    def chip_sum(x_, z_, own, other):
        slot = inverse[0, x_ * 8 + z_]
        value = jnp.where(slot > 0, own[jnp.maximum(slot - 1, 0)], 0.0)
        slot = inverse[1, x_ * 8 + z_]
        return value + jnp.where(slot > 0, other[jnp.maximum(slot - 1, 0)], 0.0)

    g_c.wait_recv()
    g_x = []
    for i, d in enumerate((2, 1, 3, 0)):
        for z_ in range(NZ):
            gs2[i, z_] = chip_sum(line_x(d), z_, grams, grams_other)
        if d:
            cp = remote(gs2.at[i], gr2.at[x], gxs.at[i], gxr.at[x], at(line_x(d), z, c))
            cp.start()
            g_x.append(cp)

    for d in (2, 1, 3):
        wait_recv(table.at[line_x(d), c], txr.at[line_x(d)])
    t_c = remote(table.at[:, c], table.at[:, c], tcs, tcr, at(x, z, 1 - c))
    t_c.start()
    for d in (2, 1, 3):
        wait_recv(gr2.at[line_x(d)], gxr.at[line_x(d)])
    for z_ in range(NZ):
        gs3[z_] = gs2[3, z_] + gr2[line_x(1), z_] + gr2[line_x(2), z_] + gr2[line_x(3), z_]
    g_z = []
    for i, d in enumerate((4, 3, 5, 2, 6, 1, 7)):
        cp = remote(
            gs3.at[line_z(d)], gr3.at[z], gzs.at[i], gzr.at[z], at(x, line_z(d), c)
        )
        cp.start()
        g_z.append(cp)

    wait_recv(table.at[:, 1 - c], tcr)
    for s in range(SLOTS):
        b = blocks[0, s]
        value = table[b // 16, lax.rem(b, 2), lax.rem(b // 2, 8)]
        chosen[s * NB : (s + 1) * NB, :] = jnp.where(
            s < live_count, value.astype(jnp.float32), 0.0
        )
    picked = jnp.transpose(chosen[...]).astype(jnp.bfloat16)

    def model_step(i, carry):
        at_ = pl.ds(pl.multiple_of(i * 512, 512), 512)
        model[:, at_] = lax.dot_general(
            picked, f_v[at_, :], (((1,), (1,)), ((), ())), preferred_element_type=jnp.float32
        )
        return carry

    lax.fori_loop(0, pixels // 512, model_step, 0)

    for pair in ((1, 7), (3, 5), (0, 4), (2, 6)):
        sources = [lax.rem(z + NZ - d, NZ) for d in pair]
        rows = [pl.ds(pl.multiple_of(zs * ROWS, ROWS), ROWS) for zs in sources]
        for zs in sources:
            wait_recv(arrived.at[zs], mr.at[zs])

        def product_step(j, acc):
            pieces = []
            for i in range(8):
                col = pl.ds(pl.multiple_of(j * 1024, 1024) + i * LANES, LANES)
                halves = []
                for half in range(2):
                    frames = arrived[sources[half], j * 8 + i].reshape(ROWS, LANES)
                    halves.append(frames.astype(jnp.float32) - model[rows[half], col])
                pieces.append(jnp.concatenate(halves, axis=0).astype(jnp.bfloat16))
            residual = jnp.concatenate(pieces, axis=1)
            at_ = pl.ds(pl.multiple_of(j * 1024, 1024), 1024)
            return acc + jnp.dot(residual, f_v[at_, :], preferred_element_type=jnp.float32)

        product = lax.fori_loop(
            0, pixels // 1024, product_step, jnp.zeros((2 * ROWS, SLOTS * NB), jnp.float32),
            unroll=True,
        )
        for half in range(2):
            products[rows[half], :] = product[half * ROWS : (half + 1) * ROWS, :]

    p_c, p_x, p_z = [], [], []
    for half in range(2):
        piece = pl.ds(half * 8, 8)
        part[piece] = jnp.transpose(
            products[:, half * LANES : (half + 1) * LANES]
        ).reshape(8, NB, LANES)
        cp = remote(
            part.at[piece], part_other.at[piece], pcs.at[half], pcr.at[half], at(x, z, 1 - c)
        )
        cp.start()
        p_c.append(cp)

    for half in range(2):
        p_c[half].wait_recv()
    far, near_z = (4, 3, 5), (2, 6, 1, 7, 0)
    p_f = []

    def send_far(d):
        j = far.index(d)
        for i, dx in enumerate((2, 1, 3, 0)):
            xd = line_x(dx)
            pf1[j, i] = chip_sum(xd, line_z(d), part, part_other)
            cp = remote(
                pf1.at[j, i], pf2.at[j, x], pfs.at[j, i], pfr.at[j, x], at(xd, line_z(d), c)
            )
            cp.start()
            p_f.append(cp)

    pieces = ((0, 2), (2, 5))

    def send_piece(h):
        lo, hi = pieces[h]
        for i, dx in enumerate((2, 1, 3)):
            xd = line_x(dx)
            for j in range(lo, hi):
                ps2[i, j] = chip_sum(xd, line_z(near_z[j]), part, part_other)
            piece = pl.ds(lo, hi - lo)
            cp = remote(
                ps2.at[i, piece], pr2.at[x, piece], pxs.at[h, i], pxr.at[h, x], at(xd, z, c)
            )
            cp.start()
            p_x.append(cp)

    send_far(4)
    send_piece(0)
    send_far(3)
    send_far(5)
    send_piece(1)
    for j in range(5):
        ps2[3, j] = chip_sum(x, line_z(near_z[j]), part, part_other)

    quotient = None
    for h, (lo, hi) in enumerate(pieces):
        for dx in (1, 3, 2):
            wait_recv(pr2.at[line_x(dx), pl.ds(lo, hi - lo)], pxr.at[h, line_x(dx)])
        for j in range(lo, hi):
            d = near_z[j]
            value = ps2[3, j]
            for dx in (1, 2, 3):
                value = value + pr2[line_x(dx), j]
            if d:
                ps3[j] = value
                cp = remote(ps3.at[j], pr3.at[z], pzs.at[j], pzr.at[z], at(x, line_z(d), c))
                cp.start()
                p_z.append(cp)
            else:
                quotient = value

    for d in range(1, NZ):
        wait_recv(gr3.at[line_z(d)], gzr.at[line_z(d)])
    packed = gs3[z]
    for d in range(1, NZ):
        packed = packed + gr3[line_z(d)]
    for half in range(2):
        wide = spread(
            jnp.where(keep, jnp.broadcast_to(packed[half : half + 1, :], (8, LANES)), 0.0)
        )
        for k in range(NB):
            column = jnp.sum(jnp.where(lane[:8] == k, wide, 0.0), axis=1, keepdims=True)
            gcol[k, half * 8 : half * 8 + 8, :] = jnp.broadcast_to(column, (8, LANES))

    for d in (1, 7, 2, 6):
        wait_recv(pr3.at[line_z(d)], pzr.at[line_z(d)])
        quotient = quotient + pr3[line_z(d)]
    for j in (1, 2, 0):
        for dx in (0, 1, 3, 2):
            wait_recv(pf2.at[j, line_x(dx)], pfr.at[j, line_x(dx)])
            quotient = quotient + pf2[j, line_x(dx)]

    previous = table[x, c, z].astype(jnp.float32)
    for k in range(NB):
        before = previous[k : k + 1, :]
        gram = gcol[k]
        updated = jnp.maximum(before + quotient[k : k + 1, :] / gram[k : k + 1, :], 0.0)
        out[k : k + 1, :] = updated
        if k + 1 < NB:
            quotient = quotient - gram * (updated - before)

    for cp in lists + t_z + t_x + [t_c, g_c] + g_x + g_z + p_c + p_x + p_z + p_f:
        cp.wait_send()

    @pl.when(x == y)
    def _():
        part_ = movie.at[pl.ds(0, 63)]
        remote(part_, part_, ms, ms, (t, y)).wait_send()

    @pl.when(x != y)
    def _():
        remote(movie, movie, ms, ms, (t, y)).wait_send()


def shards(movie_frames, footprints, tile_blocks, tile_count, traces):
    tiles_here, pixels, columns = footprints.shape
    tile_devices = lax.axis_size("tile")
    shard_rows = movie_frames.shape[0]
    movie = movie_frames.reshape(shard_rows, tile_devices, pixels // LANES, LANES)
    movie = movie.transpose(1, 2, 0, 3)
    f32, bf16 = jnp.float32, jnp.bfloat16
    dma = pltpu.SemaphoreType.DMA
    vmem = pl.BlockSpec(memory_space=pltpu.VMEM)
    hbm = pl.BlockSpec(memory_space=pl.ANY)
    tile = (NB, LANES)
    packed = (2, LANES)
    scratch = [
        pltpu.SMEM((1, SLOTS), jnp.int32),
        pltpu.SMEM((1, 1), jnp.int32),
        pltpu.SMEM((1, SLOTS), jnp.int32),
        pltpu.SMEM((1, 1), jnp.int32),
        pltpu.VMEM((pixels, columns), bf16),
        pltpu.VMEM((NZ, pixels // LANES, NC * NY, 2, LANES), bf16),
        pltpu.VMEM((LANES, pixels), f32),
        pltpu.VMEM((LANES, columns), f32),
        pltpu.VMEM((NX, NC, NZ) + tile, bf16),
        pltpu.VMEM((columns, LANES), f32),
        pltpu.VMEM((columns, columns), f32),
        pltpu.SMEM((2, NX * NZ), jnp.int32),
        pltpu.VMEM((SLOTS,) + tile, f32),
        pltpu.VMEM((SLOTS,) + tile, f32),
        pltpu.VMEM((SLOTS,) + packed, f32),
        pltpu.VMEM((SLOTS,) + packed, f32),
        pltpu.VMEM((NX, NZ) + packed, f32),
        pltpu.VMEM((NX, NZ) + packed, f32),
        pltpu.VMEM((NZ,) + packed, f32),
        pltpu.VMEM((NZ,) + packed, f32),
        pltpu.VMEM((NB,) + tile, f32),
        pltpu.VMEM((NX, 5) + tile, f32),
        pltpu.VMEM((NX, 5) + tile, f32),
        pltpu.VMEM((4,) + tile, f32),
        pltpu.VMEM((NZ,) + tile, f32),
        pltpu.VMEM((3, NX) + tile, f32),
        pltpu.VMEM((3, NX) + tile, f32),
        pltpu.SemaphoreType.REGULAR((2,)), dma, dma((3,)), dma((4,)), dma, dma((NZ,)),
        dma((7,)), dma((NZ,)), dma((3,)), dma((NX,)), dma, dma,
        dma, dma, dma((3,)), dma((NX,)), dma((7,)), dma((NZ,)),
        dma((2,)), dma((2,)), dma((2, 3)), dma((2, NX)), dma((4,)), dma((NZ,)),
        dma((3, NX)), dma((3, NX)),
    ]
    updated = pl.pallas_call(
        kernel,
        out_shape=pltpu.VMEM(tile, f32),
        in_specs=[hbm] * 5,
        out_specs=vmem,
        scratch_shapes=scratch,
        compiler_params=pltpu.CompilerParams(collective_id=1, has_side_effects=True),
        name="hals",
    )(tile_blocks, tile_count.reshape(1, 1), movie, footprints.reshape(pixels, columns), traces)
    return jnp.maximum(updated, 0.0)


def solution(mesh):
    placed = (
        P(("tile", "tm"), None),
        P("tile", None, None),
        P("tile", None),
        P("tile"),
        P("tile", "tm"),
    )
    return jax.shard_map(
        shards, mesh=mesh, in_specs=placed, out_specs=P("tile", "tm"), check_vma=False
    )
```
